1024 devices in a mesh: seq: 64 (over z, x), head: 8 (over y), pair: 2 (over core).
Axes of the slice: x: 4, y: 8, z: 16, core: 2. Of those that a mesh axis runs over, the one named last changes fastest.
Arguments:
- query_rows: bfloat16 [8192, 2048], P('seq', ('head', 'pair')), may hold values from -6 to 6
- all_head_keys: bfloat16 [8192, 2048], P('seq', ('head', 'pair')), may hold values from -6 to 6
- value_rows: bfloat16 [8192, 2048], P('seq', ('head', 'pair')), may hold values from -6 to 6
- stream: bfloat16 [8192, 2048], P(('seq', 'head', 'pair')), may hold values from -6 to 6
- attn_gain: float32 [2048], P(('head', 'pair')), may hold values from 0.5 to 2
- out_weight: bfloat16 [2048, 2048], P(('head', 'pair')), may hold values from -0.125 to 0.125
- moe_gain: float32 [2048], replicated, may hold values from 0.5 to 2
- routes: int32 [8192, 8], P(('seq', 'head')), may hold values from 0 to 127, all different within a row; in each aligned block of 8 rows (0 to 7, 8 to 15, ...) at most 2 rows name the same one
- gate_weights: float32 [8192, 8], P(('seq', 'head')), may hold values from 0.1 to 0.4
- w_gate: bfloat16 [128, 2048, 768], P('seq', None, 'pair'), may hold values from -0.125 to 0.125
- w_up: bfloat16 [128, 2048, 768], P('seq', None, 'pair'), may hold values from -0.125 to 0.125
- w_down: bfloat16 [128, 768, 2048], P('seq', 'pair'), may hold values from -0.21875 to 0.21875
Outputs:
- layer_out: bfloat16 [8192, 2048], P(('seq', 'head', 'pair'))
The draws below stay inside these ranges and needn't reach their ends.
Inputs may be any that keep to these rules, and one draw needn't show every extreme that they name: `routes`: each row names 8 different experts; within each aligned block of 8 rows no expert is named more than 2 times.
All inputs are finite; a program needn't handle non-finite values.
Results may differ from the reference program's by a relative error of at most 0.018.
Values may be sent and summed in bfloat16 or wider, within the bound.
No kernel may reach another device: no remote copies, remote signals or barrier semaphores. Data moves between devices by JAX's collectives and lax.ppermute only.
A program may use at most 64 MiB of HBM per device.

```python
import math
import jax
import jax.numpy as jnp
import numpy as np
from jax import lax

D = 2048
HEADS = 16
HEAD_DIM = 128
HID = 768
TOP = 8
TOK_DEV = 128
EXPERTS = 128
TOKENS = 8192
MOE_ROWS = 8
CAP = 2


def level_of(rng, extent, split, low, high):
    loudness = 1.0
    for position, blocks in split:
        heights = jax.random.uniform(jax.random.fold_in(jax.random.fold_in(rng, 6), position), (blocks,), jnp.float32, low / len(split), high / len(split))
        loudness = loudness * jnp.repeat(jnp.exp(heights), extent[position] // blocks).reshape((-1,) + (1,) * (len(extent) - 1 - position))
    return loudness


def shared_out(own_key, own, number, rows, count, top, bound, skew):
    order = jax.random.permutation(own_key, count)
    crowded, ordinary = shares(count, rows * top, bound, skew, True), shares(count, rows * top, bound, skew, False)
    places = jnp.arange(count)

    def named(lengths, turn):
        used = int((lengths > 0).sum())
        fixed = max(1, used // 4)
        shifted = fixed + (places - fixed + turn * (used - fixed)) % max(1, count - fixed)
        return jnp.zeros((count,), jnp.int32).at[order[jnp.where(places < fixed, places, shifted)]].set(jnp.asarray(lengths, jnp.int32))

    lengths = jnp.where(number % 4 == 0, named(crowded, number // 4), named(ordinary, number - number // 4 - 1))
    mixed = jax.random.permutation(jax.random.fold_in(own, 3), count)
    source_of, receiver = mixed[0:count // 2 * 2:2], mixed[1:count // 2 * 2:2]
    slack = jnp.minimum(lengths[source_of] - 1, bound - lengths[receiver]) // 2
    slack = jnp.where((source_of == order[0]) | (receiver == order[0]) | (lengths[receiver] == 0), 0, jnp.maximum(slack, 0))
    shifted = jax.random.randint(jax.random.fold_in(own, 4), (count // 2,), 0, 1 << 20) % (slack + 1)
    lengths = lengths.at[source_of].add(-shifted).at[receiver].add(shifted)
    items = jnp.searchsorted(jnp.cumsum(lengths), jnp.arange(rows * top), side="right").astype(jnp.int32)
    table = items.reshape(top, rows).T
    table = table[jax.random.permutation(jax.random.fold_in(own, 1), rows)]
    turn = jax.random.randint(jax.random.fold_in(own, 2), (rows, 1), 0, top)
    return jnp.take_along_axis(table, (jnp.arange(top)[None, :] + turn) % top, axis=1)


def shares(amount, total, reach, lean, full):
    weights = [(1 << 20) // math.isqrt(rank ** lean) + 1 for rank in range(1, amount + 1)]
    largest = reach if full else min(reach, max(-(-total // amount), total * weights[0] // sum(weights)))
    least = 1 if total - largest >= amount - 1 else 0
    holding, spare = [largest] + [least] * (amount - 1), total - largest - least * (amount - 1)
    while spare > 0:
        free = [i for i in range(1, amount) if holding[i] < largest] or [i for i in range(1, amount) if holding[i] < reach]
        pool, budget = sum([weights[i] for i in free]), spare
        for i in free:
            more = min(reach - holding[i], max(1, budget * weights[i] // pool), spare)
            holding[i] = holding[i] + more
            spare = spare - more
    return np.array(holding)


def bell_draw(rng, shape, deviation, reach, cuts=(), kind=jnp.bfloat16):
    drawn = deviation * jax.random.normal(rng, shape, jnp.float32)
    if cuts:
        drawn = drawn * level_of(rng, shape, cuts, -0.22, 0.18)
    return jnp.clip(drawn, -reach, reach).astype(kind)


def setup_inputs(seed: int = 0) -> dict:
    streams_of = jax.random.split(jax.random.key(seed), 13)
    query_rows = bell_draw(streams_of[0], (TOKENS, HEADS * HEAD_DIM), 1.0, 6.0, ((0, 64), (1, 16)))
    all_head_keys = bell_draw(streams_of[1], (TOKENS, HEADS * HEAD_DIM), 1.0, 6.0, ((0, 64), (1, 16)))
    value_rows = bell_draw(streams_of[2], (TOKENS, HEADS * HEAD_DIM), 1.0, 6.0, ((0, 64), (1, 16)))
    stream = bell_draw(streams_of[3], (TOKENS, D), 1.0, 6.0, ((0, 1024),))
    attn_gain = jnp.clip(jnp.exp(math.log(2.0) - 1.3862944 * jax.random.uniform(streams_of[4], (HEADS * HEAD_DIM,), jnp.float32) ** level_of(streams_of[4], (HEADS * HEAD_DIM,), ((0, 16),), -0.2, 0.2)), 0.5, 2.0)
    out_weight = bell_draw(streams_of[5], (HEADS * HEAD_DIM, D), (HEADS * HEAD_DIM) ** -0.5, 0.125, ((0, 16),))
    moe_gain = jnp.clip(jnp.exp(jax.random.uniform(streams_of[6], (D,), jnp.float32, math.log(0.5), math.log(2.0))), 0.5, 2.0)
    routes_keys = jax.random.split(jax.random.fold_in(streams_of[7], 1), TOKENS // MOE_ROWS)
    routes_turns = jax.random.permutation(jax.random.fold_in(streams_of[7], 3), TOKENS // MOE_ROWS)
    routes = jax.vmap(lambda own, number: shared_out(jax.random.fold_in(streams_of[7], 2), own, number, MOE_ROWS, EXPERTS, TOP, CAP, 2))(routes_keys, routes_turns).reshape((TOKENS, TOP))
    gate_weights = jnp.clip(0.1 + 0.3 * jax.random.uniform(streams_of[8], (TOKENS, TOP), jnp.float32) ** level_of(streams_of[8], (TOKENS, TOP), ((0, 512),), -0.2, 0.2), 0.1, 0.4)
    w_gate = bell_draw(streams_of[9], (EXPERTS, D, HID), D ** -0.5, 0.125, ((0, 64), (2, 2)))
    w_up = bell_draw(streams_of[10], (EXPERTS, D, HID), D ** -0.5, 0.125, ((0, 64), (2, 2)))
    w_down = bell_draw(streams_of[11], (EXPERTS, HID, D), HID ** -0.5, 0.21875, ((0, 64), (1, 2)))
    return {"query_rows": query_rows, "all_head_keys": all_head_keys, "value_rows": value_rows, "stream": stream, "attn_gain": attn_gain, "out_weight": out_weight, "moe_gain": moe_gain, "routes": routes, "gate_weights": gate_weights, "w_gate": w_gate, "w_up": w_up, "w_down": w_down}


MAXIMUM_ACCURACY = lax.Precision.HIGHEST
EPSILON = 1e-06

def rms_scale(values, gain_vec):
    mean_sq = lax.optimization_barrier(jnp.mean(values * values, axis=-1, keepdims=True))
    return values * lax.rsqrt(mean_sq + EPSILON) * gain_vec

def slot_ranks(expert_ids, num_experts):
    flat_ids = expert_ids.reshape(-1)
    one_hot = (flat_ids[:, None] == jnp.arange(num_experts, dtype=jnp.int32)[None, :]).astype(jnp.int32)
    before = jnp.cumsum(one_hot, axis=0) - one_hot
    return lax.optimization_barrier(jnp.sum(before * one_hot, axis=1)).astype(jnp.int32)

def head_attention(query_head, key_head, value_head):
    blocks = TOKENS // TOK_DEV
    query_blocks = query_head.reshape(blocks, TOK_DEV, HEAD_DIM)
    key_blocks = key_head.reshape(blocks, TOK_DEV, HEAD_DIM)
    value_blocks = value_head.reshape(blocks, TOK_DEV, HEAD_DIM)
    causal = (jnp.arange(TOK_DEV)[:, None] >= jnp.arange(TOK_DEV)[None, :]).astype(jnp.float32)

    def advance(carried, block_parts):
        query_part, key_part, value_part = block_parts
        scores = jnp.dot(query_part, key_part.T, precision=MAXIMUM_ACCURACY) * causal
        result = jnp.dot(scores, value_part, precision=MAXIMUM_ACCURACY) + jnp.dot(query_part, carried, precision=MAXIMUM_ACCURACY)
        carried = carried + jnp.dot(key_part.T, value_part, precision=MAXIMUM_ACCURACY)
        return (carried, result)
    start_state = jnp.zeros((HEAD_DIM, HEAD_DIM), jnp.float32)
    _, results = lax.scan(advance, start_state, (query_blocks, key_blocks, value_blocks))
    return results.reshape(TOKENS, HEAD_DIM)

def attend(head_parts):
    return head_attention(head_parts[0], head_parts[1], head_parts[2])

def rank_block(expert_block):
    return slot_ranks(expert_block, EXPERTS)

def split_heads(matrix):
    return matrix.astype(jnp.float32).reshape(TOKENS, HEADS, HEAD_DIM).transpose(1, 0, 2)

def reference(query_rows, all_head_keys, value_rows, stream, attn_gain, out_weight, moe_gain, routes, gate_weights, w_gate, w_up, w_down):
    mixed = lax.map(attend, (split_heads(query_rows), split_heads(all_head_keys), split_heads(value_rows)))
    normed = rms_scale(mixed, attn_gain.reshape(HEADS, 1, HEAD_DIM))
    attn_normed = normed.transpose(1, 0, 2).reshape(TOKENS, HEADS * HEAD_DIM).astype(jnp.bfloat16)
    residual = stream.astype(jnp.float32) + jnp.dot(attn_normed, out_weight, preferred_element_type=jnp.float32)
    moe_input = rms_scale(residual, moe_gain).astype(jnp.bfloat16)
    blocks = TOKENS // MOE_ROWS
    ranks = jax.vmap(rank_block)(routes.reshape(blocks, MOE_ROWS, TOP))
    expert_ids = routes.reshape(blocks, MOE_ROWS * TOP)
    slot_pos = jnp.arange(blocks, dtype=jnp.int32)[:, None] * CAP + ranks
    token_ids = jnp.repeat(jnp.arange(TOKENS, dtype=jnp.int32).reshape(blocks, MOE_ROWS), TOP, axis=1)
    token_table = jnp.full((EXPERTS, blocks * CAP), TOKENS, jnp.int32)
    token_table = token_table.at[expert_ids.reshape(-1), slot_pos.reshape(-1)].set(token_ids.reshape(-1))
    weight_table = jnp.zeros((EXPERTS, blocks * CAP), jnp.float32)
    weight_table = weight_table.at[expert_ids.reshape(-1), slot_pos.reshape(-1)].set(gate_weights.reshape(-1))
    padded_input = jnp.concatenate([moe_input, jnp.zeros((1, D), jnp.bfloat16)], axis=0)

    def expert_pass(total, expert_parts):
        token_slots, slot_weights, gate_mat, up_mat, down_mat = expert_parts
        inputs = padded_input[token_slots]
        gate_part = jnp.dot(inputs, gate_mat, preferred_element_type=jnp.float32)
        up_part = jnp.dot(inputs, up_mat, preferred_element_type=jnp.float32)
        activated = (jax.nn.silu(gate_part) * up_part).astype(jnp.bfloat16)
        expert_out = jnp.dot(activated, down_mat, preferred_element_type=jnp.float32).astype(jnp.bfloat16)
        total = total.at[token_slots].add(slot_weights[:, None] * expert_out.astype(jnp.float32))
        return (total, None)
    start_total = jnp.zeros((TOKENS + 1, D), jnp.float32)
    total, _ = lax.scan(expert_pass, start_total, (token_table, weight_table, w_gate, w_up, w_down))
    return (residual + total[:TOKENS]).astype(jnp.bfloat16)
```

```python
import jax
import jax.numpy as jnp
from jax import lax
from jax.sharding import Mesh
from jax.sharding import PartitionSpec as P

HEAD_DIM = 128
LANES = 128
ROUTE_BLOCK = 8
SEQ = ("seq_0", "seq_1")
SEQ_HEAD_PAIR = ("seq_0", "seq_1", "head", "pair")
SEQ_HEAD = ("seq_0", "seq_1", "head")
EPSILON = 1e-06


def rms_scale(values, gain_vec):
    mean_sq = jnp.mean(values * values, axis=-1, keepdims=True)
    return values * lax.rsqrt(mean_sq + EPSILON) * gain_vec


def entering_state(local_state):
    size = lax.axis_size(SEQ)
    rows, width = local_state.shape
    pieces = local_state.astype(jnp.bfloat16).reshape(size, rows // size, width)
    gathered = lax.all_to_all(pieces, SEQ, 0, 0, tiled=True)
    place = jnp.arange(size)
    earlier = (place[:, None] > place[None, :]).astype(jnp.bfloat16)
    sums = jnp.dot(
        earlier, gathered.reshape(size, -1), preferred_element_type=jnp.float32
    )
    back = lax.all_to_all(
        sums.astype(jnp.bfloat16).reshape(pieces.shape), SEQ, 0, 0, tiled=True
    )
    return back.reshape(rows, width)


def with_routing(rows, expert_ids, weights):
    count, top = expert_ids.shape
    high = weights.astype(jnp.bfloat16)
    low = (weights - high.astype(jnp.float32)).astype(jnp.bfloat16)
    tail = jnp.concatenate(
        [
            expert_ids.astype(jnp.bfloat16),
            high,
            low,
            jnp.zeros((count, LANES - 3 * top), jnp.bfloat16),
        ],
        axis=1,
    )
    return jnp.concatenate([rows, tail], axis=1)


def body(
    query_rows,
    all_head_keys,
    value_rows,
    stream,
    attn_gain,
    out_weight,
    moe_gain,
    routes,
    gate_weights,
    w_gate,
    w_up,
    w_down,
):
    length = query_rows.shape[0]
    local_state = jnp.einsum(
        "tz,td->zd", all_head_keys, value_rows, preferred_element_type=jnp.float32
    )
    previous = entering_state(local_state)
    causal = jnp.arange(length)[:, None] >= jnp.arange(length)[None, :]
    scores = jnp.where(
        causal,
        jnp.einsum("tk,sk->ts", query_rows, all_head_keys, preferred_element_type=jnp.float32),
        0.0,
    )
    mixed = jnp.dot(scores, value_rows.astype(jnp.float32))
    mixed = mixed + jnp.dot(query_rows, previous, preferred_element_type=jnp.float32)
    attn_normed = rms_scale(mixed, attn_gain[None, :]).astype(jnp.bfloat16)
    partial_rows = jnp.dot(attn_normed, out_weight, preferred_element_type=jnp.float32)
    projected = lax.psum_scatter(
        partial_rows.astype(jnp.bfloat16), ("head", "pair"), scatter_dimension=0, tiled=True
    )
    block_rows, model_width = stream.shape
    residual = stream.astype(jnp.float32) + projected.astype(jnp.float32)
    moe_input = rms_scale(residual, moe_gain).astype(jnp.bfloat16)

    core = lax.axis_index("pair")
    my_routes = lax.dynamic_slice_in_dim(routes, core * block_rows, block_rows, 0)
    my_weights = lax.dynamic_slice_in_dim(gate_weights, core * block_rows, block_rows, 0)
    packed = with_routing(moe_input, my_routes, my_weights)
    plane = lax.all_gather(packed, SEQ, tiled=True)
    plane = lax.all_gather(plane, "pair", tiled=True)
    tokens = plane[:, :model_width]
    routing = plane[:, model_width:].astype(jnp.float32)
    top = routes.shape[1]
    ids = routing[:, :top]
    weights = routing[:, top : 2 * top] + routing[:, 2 * top : 3 * top]

    experts_here = w_gate.shape[0]
    first = lax.axis_index(SEQ) * experts_here
    hidden = []
    for expert in range(experts_here):
        named = ids == (first + expert).astype(jnp.float32)
        weight = jnp.sum(jnp.where(named, weights, 0.0), axis=1, keepdims=True)
        gate_part = jnp.dot(tokens, w_gate[expert], preferred_element_type=jnp.float32)
        up_part = jnp.dot(tokens, w_up[expert], preferred_element_type=jnp.float32)
        hidden.append((jax.nn.silu(gate_part) * up_part * weight).astype(jnp.bfloat16))
    outputs = jnp.dot(
        jnp.concatenate(hidden, axis=1),
        w_down.reshape(-1, model_width),
        preferred_element_type=jnp.float32,
    ).astype(jnp.bfloat16)
    outputs = lax.psum_scatter(outputs, "pair", scatter_dimension=0, tiled=True)
    combined = lax.psum_scatter(outputs, SEQ, scatter_dimension=0, tiled=True)
    return (residual + combined.astype(jnp.float32)).astype(jnp.bfloat16)


def solution(mesh):
    split = Mesh(
        mesh.devices.reshape(16, 4, mesh.shape["head"], mesh.shape["pair"]),
        ("seq_0", "seq_1", "head", "pair"),
    )
    placed = (
        P(SEQ, ("head", "pair")),
        P(SEQ, ("head", "pair")),
        P(SEQ, ("head", "pair")),
        P(SEQ_HEAD_PAIR, None),
        P(("head", "pair")),
        P(("head", "pair"), None),
        P(),
        P(SEQ_HEAD, None),
        P(SEQ_HEAD, None),
        P(SEQ, None, "pair"),
        P(SEQ, None, "pair"),
        P(SEQ, "pair", None),
    )
    return jax.shard_map(
        body, mesh=split, in_specs=placed, out_specs=P(SEQ_HEAD_PAIR, None), check_vma=False
    )
```

```python
import jax
import jax.numpy as jnp
from jax import lax
from jax.sharding import Mesh
from jax.sharding import PartitionSpec as P

LANES = 128
CAP = 2
Z = ("zh", "zl")
NEAR = ("zl", "x")
SEQ = ("zh", "zl", "x")
SEQ_HEAD_PAIR = ("zh", "zl", "x", "head", "pair")
SEQ_HEAD = ("zh", "zl", "x", "head")
SWAP = ((0, 1), (1, 0))
EPSILON = 1e-06


def rms_scale(values, gain_vec):
    mean_sq = jnp.mean(values * values, axis=-1, keepdims=True)
    return values * lax.rsqrt(mean_sq + EPSILON) * gain_vec


def to_each(shard, axis):
    copies = jnp.broadcast_to(shard[None], (lax.axis_size(axis), *shard.shape))
    return lax.all_to_all(copies, axis, 0, 0, tiled=True)


def entering_state(local_state):
    rows, width = local_state.shape
    across = lax.axis_size("x")
    along = lax.axis_size(Z)
    parts = local_state.astype(jnp.bfloat16).reshape(across, rows // across, width)
    parts = lax.all_to_all(parts, "x", 0, 0, tiled=True).astype(jnp.float32)
    totals = to_each(jnp.sum(parts, axis=0).astype(jnp.bfloat16), Z).astype(jnp.float32)
    passed = (jnp.arange(along) < lax.axis_index(Z))[:, None, None]
    running = jnp.sum(jnp.where(passed, totals, 0.0), axis=0)
    entering = []
    for place in range(across):
        entering.append(running.astype(jnp.bfloat16))
        running = running + parts[place]
    back = lax.all_to_all(jnp.stack(entering), "x", 0, 0, tiled=True)
    return back.reshape(rows, width)


def two_terms(values):
    high = lax.reduce_precision(values, exponent_bits=8, mantissa_bits=7)
    return high.astype(jnp.bfloat16), (values - high).astype(jnp.bfloat16)


def with_routing(rows, expert_ids, weights):
    count, top = expert_ids.shape
    high, low = two_terms(weights)
    tail = jnp.concatenate(
        [
            expert_ids.astype(jnp.bfloat16),
            high,
            low,
            jnp.zeros((count, LANES - 3 * top), jnp.bfloat16),
        ],
        axis=1,
    )
    return jnp.concatenate([rows, tail], axis=1)


def slot_matrices(ids, weights, first, experts, block_rows):
    count = ids.shape[0]
    blocks = count // block_rows
    wanted = first + jnp.arange(experts, dtype=jnp.int32)
    named = wanted.astype(jnp.float32)[:, None, None] == ids.T[None]
    chosen = jnp.sum(named.astype(jnp.float32), axis=1)
    weight = jnp.sum(jnp.where(named, weights.T[None], 0.0), axis=1)
    row = jnp.arange(count)
    same_block = row[:, None] // block_rows == row[None, :] // block_rows
    ahead = (same_block & (row[:, None] < row[None, :])).astype(jnp.bfloat16)
    rank = jnp.dot(chosen.astype(jnp.bfloat16), ahead, preferred_element_type=jnp.float32)
    code = jnp.where(chosen > 0.0, rank, -1.0)
    per_expert = blocks * CAP
    slot = jnp.arange(per_expert)
    in_block = slot[:, None] // CAP == row[None, :] // block_rows
    slot_rank = (slot % CAP).astype(jnp.float32)
    fills = in_block[None] & (code[:, None, :] == slot_rank[None, :, None])
    fills = fills.reshape(experts * per_expert, count)
    added = jnp.broadcast_to(weight[:, None, :], (experts, per_expert, count))
    added = jnp.where(fills, added.reshape(fills.shape), 0.0)
    return fills.astype(jnp.bfloat16), added


def body(
    query_rows,
    all_head_keys,
    value_rows,
    stream,
    attn_gain,
    out_weight,
    moe_gain,
    routes,
    gate_weights,
    w_gate,
    w_up,
    w_down,
):
    length, head_width = query_rows.shape
    block_rows, model_width = stream.shape
    heads = lax.axis_size("head")
    core = lax.axis_index("pair")
    other_weight = lax.ppermute(out_weight, "pair", SWAP)

    local_state = jnp.einsum(
        "tz,td->zd", all_head_keys, value_rows, preferred_element_type=jnp.float32
    )
    previous = entering_state(local_state)
    causal = jnp.arange(length)[:, None] >= jnp.arange(length)[None, :]
    scores = jnp.where(
        causal,
        jnp.einsum("tk,sk->ts", query_rows, all_head_keys, preferred_element_type=jnp.float32),
        0.0,
    )
    mixed = jnp.dot(scores, value_rows.astype(jnp.float32))
    mixed = mixed + jnp.dot(query_rows, previous, preferred_element_type=jnp.float32)
    attn_normed = rms_scale(mixed, attn_gain[None, :]).astype(jnp.bfloat16)

    by_core = attn_normed.reshape(heads, 2, block_rows, head_width)
    kept = jnp.where(core == 0, by_core[:, 0], by_core[:, 1]).reshape(-1, head_width)
    given = jnp.where(core == 0, by_core[:, 1], by_core[:, 0]).reshape(-1, head_width)
    taken = lax.ppermute(given, "pair", SWAP)
    partial_rows = jnp.dot(kept, out_weight, preferred_element_type=jnp.float32) + jnp.dot(
        taken, other_weight, preferred_element_type=jnp.float32
    )
    partial_rows = partial_rows.astype(jnp.bfloat16).reshape(heads, block_rows, model_width)
    partial_rows = lax.all_to_all(partial_rows, "head", 0, 0, tiled=True)
    projected = jnp.sum(partial_rows.astype(jnp.float32), axis=0)
    residual = stream.astype(jnp.float32) + projected
    moe_input = rms_scale(residual, moe_gain).astype(jnp.bfloat16)

    top = routes.shape[1]
    my_routes = lax.dynamic_slice_in_dim(routes, core * block_rows, block_rows, 0)
    my_weights = lax.dynamic_slice_in_dim(gate_weights, core * block_rows, block_rows, 0)
    packed = to_each(with_routing(moe_input, my_routes, my_weights), "zh")
    blocks = packed.shape[0]
    packed = packed.reshape(blocks * block_rows, -1)
    routing = packed[:, model_width : model_width + 3 * top].astype(jnp.float32)
    weights = routing[:, top : 2 * top] + routing[:, 2 * top :]
    experts_here = w_gate.shape[0]
    near = lax.axis_size(NEAR)
    fills, added = slot_matrices(
        routing[:, :top],
        weights,
        lax.axis_index("zh") * near * experts_here,
        near * experts_here,
        block_rows,
    )
    slots = jnp.dot(fills, packed[:, :model_width], preferred_element_type=jnp.float32)
    slots = slots.astype(jnp.bfloat16).reshape(near, -1, model_width)
    own = lax.all_to_all(slots, NEAR, 0, 0, tiled=True)
    other = lax.ppermute(own, "pair", SWAP)

    per_expert = blocks * CAP
    for_own, for_other = [], []
    for expert in range(experts_here):
        span = slice(expert * per_expert, (expert + 1) * per_expert)
        rows = jnp.concatenate(
            [own[:, span].reshape(-1, model_width), other[:, span].reshape(-1, model_width)]
        )
        gate_part = jnp.dot(rows, w_gate[expert], preferred_element_type=jnp.float32)
        up_part = jnp.dot(rows, w_up[expert], preferred_element_type=jnp.float32)
        activated = (jax.nn.silu(gate_part) * up_part).astype(jnp.bfloat16)
        result = jnp.dot(activated, w_down[expert], preferred_element_type=jnp.float32)
        half = near * per_expert
        for_own.append(result[:half].reshape(near, per_expert, model_width))
        for_other.append(
            result[half:].astype(jnp.bfloat16).reshape(near, per_expert, model_width)
        )
    from_other = lax.ppermute(jnp.concatenate(for_other, axis=1), "pair", SWAP)
    expert_out = jnp.concatenate(for_own, axis=1) + from_other.astype(jnp.float32)
    returned = lax.all_to_all(expert_out.astype(jnp.bfloat16), NEAR, 0, 0, tiled=True)
    returned = returned.reshape(-1, model_width)

    high, low = two_terms(added)
    sums = jnp.einsum("sr,sd->rd", high, returned, preferred_element_type=jnp.float32)
    sums = sums + jnp.einsum("sr,sd->rd", low, returned, preferred_element_type=jnp.float32)
    sums = sums.astype(jnp.bfloat16).reshape(blocks, block_rows, model_width)
    sums = lax.all_to_all(sums, "zh", 0, 0, tiled=True)
    combined = jnp.sum(sums.astype(jnp.float32), axis=0)
    return (residual + combined).astype(jnp.bfloat16)


def solution(mesh):
    split = Mesh(
        mesh.devices.reshape(8, 2, 4, mesh.shape["head"], mesh.shape["pair"]),
        SEQ_HEAD_PAIR,
    )
    placed = (
        P(SEQ, ("head", "pair")),
        P(SEQ, ("head", "pair")),
        P(SEQ, ("head", "pair")),
        P(SEQ_HEAD_PAIR, None),
        P(("head", "pair")),
        P(("head", "pair"), None),
        P(),
        P(SEQ_HEAD, None),
        P(SEQ_HEAD, None),
        P(SEQ, None, "pair"),
        P(SEQ, None, "pair"),
        P(SEQ, "pair", None),
    )
    return jax.shard_map(
        body, mesh=split, in_specs=placed, out_specs=P(SEQ_HEAD_PAIR, None), check_vma=False
    )
```

```python
import jax
import jax.numpy as jnp
from jax import lax
from jax.experimental import pallas as pl
from jax.experimental.pallas import tpu as pltpu
from jax.sharding import Mesh
from jax.sharding import PartitionSpec as P

LANES = 128
CAP = 2
Z = ("zh", "zl")
NEAR = ("zl", "x", "pair")
SEQ = ("zh", "zl", "x")
SEQ_HEAD_PAIR = ("zh", "zl", "x", "head", "pair")
SEQ_HEAD = ("zh", "zl", "x", "head")
SWAP = ((0, 1), (1, 0))
EPSILON = 1e-06


def rms_scale(values, gain_vec):
    mean_sq = jnp.mean(values * values, axis=-1, keepdims=True)
    return values * lax.rsqrt(mean_sq + EPSILON) * gain_vec


def to_each(shard, axis):
    copies = jnp.broadcast_to(shard[None], (lax.axis_size(axis), *shard.shape))
    return lax.all_to_all(copies, axis, 0, 0, tiled=True)


def entering_state(local_state):
    rows, width = local_state.shape
    across = lax.axis_size("x")
    along = lax.axis_size(Z)
    parts = local_state.astype(jnp.bfloat16).reshape(across, rows // across, width)
    parts = lax.all_to_all(parts, "x", 0, 0, tiled=True).astype(jnp.float32)
    totals = to_each(jnp.sum(parts, axis=0).astype(jnp.bfloat16), Z).astype(jnp.float32)
    passed = (jnp.arange(along) < lax.axis_index(Z))[:, None, None]
    running = jnp.sum(jnp.where(passed, totals, 0.0), axis=0)
    entering = []
    for place in range(across):
        entering.append(running.astype(jnp.bfloat16))
        running = running + parts[place]
    back = lax.all_to_all(jnp.stack(entering), "x", 0, 0, tiled=True)
    return back.reshape(rows, width)


def two_terms(values):
    high = lax.reduce_precision(values, exponent_bits=8, mantissa_bits=7)
    return high.astype(jnp.bfloat16), (values - high).astype(jnp.bfloat16)


def with_routing(rows, expert_ids, weights):
    count, top = expert_ids.shape
    high, low = two_terms(weights)
    tail = jnp.concatenate(
        [
            expert_ids.astype(jnp.bfloat16),
            high,
            low,
            jnp.zeros((count, LANES - 3 * top), jnp.bfloat16),
        ],
        axis=1,
    )
    return jnp.concatenate([rows, tail], axis=1)


def slot_matrices(ids, weights, first, experts, block_rows):
    count = ids.shape[0]
    blocks = count // block_rows
    wanted = first + jnp.arange(experts, dtype=jnp.int32)
    named = wanted.astype(jnp.float32)[:, None, None] == ids.T[None]
    chosen = jnp.sum(named.astype(jnp.float32), axis=1)
    weight = jnp.sum(jnp.where(named, weights.T[None], 0.0), axis=1)
    row = jnp.arange(count)
    same_block = row[:, None] // block_rows == row[None, :] // block_rows
    ahead = (same_block & (row[:, None] < row[None, :])).astype(jnp.bfloat16)
    rank = jnp.dot(chosen.astype(jnp.bfloat16), ahead, preferred_element_type=jnp.float32)
    code = jnp.where(chosen > 0.0, rank, -1.0)
    per_expert = blocks * CAP
    slot = jnp.arange(per_expert)
    in_block = slot[:, None] // CAP == row[None, :] // block_rows
    slot_rank = (slot % CAP).astype(jnp.float32)
    fills = in_block[None] & (code[:, None, :] == slot_rank[None, :, None])
    fills = fills.reshape(experts * per_expert, count)
    added = jnp.broadcast_to(weight[:, None, :], (experts, per_expert, count))
    added = jnp.where(fills, added.reshape(fills.shape), 0.0)
    return fills.astype(jnp.bfloat16), added


def expert_kernel(core, rows, g0, u0, d0, g1, u1, d1, out, gate_all, up_all, down_all, sems):
    mine = core[0]
    half = g0.shape[2]
    copies = []
    for place, (parts, whole) in enumerate(
        (((g0, g1), gate_all), ((u0, u1), up_all), ((d0, d1), down_all))
    ):
        for index, part in enumerate(parts):
            span = pl.ds(index * half, half)
            view = whole.at[span, :] if whole is down_all else whole.at[:, span]
            copies.append(pltpu.make_async_copy(part.at[mine], view, sems.at[place, index]))
    for copy in copies:
        copy.start()
    values = rows[...]
    copies[0].wait()
    copies[1].wait()
    gate_part = jnp.dot(values, gate_all[...], preferred_element_type=jnp.float32)
    copies[2].wait()
    copies[3].wait()
    up_part = jnp.dot(values, up_all[...], preferred_element_type=jnp.float32)
    hidden = (gate_part / (1.0 + jnp.exp(-gate_part)) * up_part).astype(jnp.bfloat16)
    copies[4].wait()
    copies[5].wait()
    result = jnp.dot(hidden, down_all[...], preferred_element_type=jnp.float32)
    out[...] = result.astype(out.dtype)


def expert(core, rows, own_parts, other_parts):
    _, width, half = own_parts[0].shape
    parts = [
        pltpu.with_memory_space_constraint(part, pltpu.HBM) for part in (*own_parts, *other_parts)
    ]
    in_place = [pl.BlockSpec(memory_space=pl.ANY)] * 6
    return pl.pallas_call(
        expert_kernel,
        out_shape=jax.ShapeDtypeStruct(rows.shape, jnp.bfloat16),
        in_specs=[
            pl.BlockSpec(memory_space=pltpu.SMEM),
            pl.BlockSpec(memory_space=pltpu.VMEM),
            *in_place,
        ],
        out_specs=pl.BlockSpec(memory_space=pltpu.VMEM),
        scratch_shapes=[
            pltpu.VMEM((width, 2 * half), jnp.bfloat16),
            pltpu.VMEM((width, 2 * half), jnp.bfloat16),
            pltpu.VMEM((2 * half, width), jnp.bfloat16),
            pltpu.SemaphoreType.DMA((3, 2)),
        ],
        compiler_params=pltpu.CompilerParams(vmem_limit_bytes=24 * 1024 * 1024),
        name="expert",
    )(core.reshape(1).astype(jnp.int32), rows, *parts)


def body(
    query_rows,
    all_head_keys,
    value_rows,
    stream,
    attn_gain,
    out_weight,
    moe_gain,
    routes,
    gate_weights,
    w_gate,
    w_up,
    w_down,
):
    length, head_width = query_rows.shape
    block_rows, model_width = stream.shape
    heads = lax.axis_size("head")
    core = lax.axis_index("pair")
    other_weight = lax.ppermute(out_weight, "pair", SWAP)
    other_parts = [lax.ppermute(part, "pair", SWAP) for part in (w_gate, w_up, w_down)]

    local_state = jnp.einsum(
        "tz,td->zd", all_head_keys, value_rows, preferred_element_type=jnp.float32
    )
    previous, other_parts[0] = lax.optimization_barrier(
        (entering_state(local_state), other_parts[0])
    )
    causal = jnp.arange(length)[:, None] >= jnp.arange(length)[None, :]
    scores = jnp.where(
        causal,
        jnp.einsum("tk,sk->ts", query_rows, all_head_keys, preferred_element_type=jnp.float32),
        0.0,
    )
    mixed = jnp.dot(scores, value_rows.astype(jnp.float32))
    mixed = mixed + jnp.dot(query_rows, previous, preferred_element_type=jnp.float32)
    attn_normed = rms_scale(mixed, attn_gain[None, :]).astype(jnp.bfloat16)

    by_core = attn_normed.reshape(heads, 2, block_rows, head_width)
    kept = jnp.where(core == 0, by_core[:, 0], by_core[:, 1]).reshape(-1, head_width)
    given = jnp.where(core == 0, by_core[:, 1], by_core[:, 0]).reshape(-1, head_width)
    taken = lax.ppermute(given, "pair", SWAP)
    partial_rows = jnp.dot(kept, out_weight, preferred_element_type=jnp.float32) + jnp.dot(
        taken, other_weight, preferred_element_type=jnp.float32
    )
    partial_rows = partial_rows.astype(jnp.bfloat16).reshape(heads, block_rows, model_width)
    partial_rows = lax.all_to_all(partial_rows, "head", 0, 0, tiled=True)
    projected = jnp.sum(partial_rows.astype(jnp.float32), axis=0)
    residual = stream.astype(jnp.float32) + projected
    moe_input = rms_scale(residual, moe_gain).astype(jnp.bfloat16)

    top = routes.shape[1]
    my_routes = lax.dynamic_slice_in_dim(routes, core * block_rows, block_rows, 0)
    my_weights = lax.dynamic_slice_in_dim(gate_weights, core * block_rows, block_rows, 0)
    packed = to_each(with_routing(moe_input, my_routes, my_weights), "zh")
    blocks = packed.shape[0]
    packed = packed.reshape(blocks * block_rows, -1)
    routing = packed[:, model_width : model_width + 3 * top].astype(jnp.float32)
    weights = routing[:, top : 2 * top] + routing[:, 2 * top :]
    near = lax.axis_size(NEAR)
    fills, added = slot_matrices(
        routing[:, :top], weights, lax.axis_index("zh") * near, near, block_rows
    )
    slots = jnp.dot(fills, packed[:, :model_width], preferred_element_type=jnp.float32)
    slots = slots.astype(jnp.bfloat16).reshape(near, -1, model_width)
    slots, *other_parts[1:] = lax.optimization_barrier((slots, *other_parts[1:]))
    rows = lax.all_to_all(slots, NEAR, 0, 0, tiled=True).reshape(-1, model_width)

    expert_out = expert(core, rows, (w_gate, w_up, w_down), other_parts).reshape(slots.shape)
    returned = lax.all_to_all(expert_out, NEAR, 0, 0, tiled=True)
    returned = returned.reshape(-1, model_width)

    high, low = two_terms(added)
    sums = jnp.einsum("sr,sd->rd", high, returned, preferred_element_type=jnp.float32)
    sums = sums + jnp.einsum("sr,sd->rd", low, returned, preferred_element_type=jnp.float32)
    sums = sums.astype(jnp.bfloat16).reshape(blocks, block_rows, model_width)
    sums = lax.all_to_all(sums, "zh", 0, 0, tiled=True)
    combined = jnp.sum(sums.astype(jnp.float32), axis=0)
    return (residual + combined).astype(jnp.bfloat16)


def solution(mesh):
    split = Mesh(
        mesh.devices.reshape(8, 2, 4, mesh.shape["head"], mesh.shape["pair"]),
        SEQ_HEAD_PAIR,
    )
    placed = (
        P(SEQ, ("head", "pair")),
        P(SEQ, ("head", "pair")),
        P(SEQ, ("head", "pair")),
        P(SEQ_HEAD_PAIR, None),
        P(("head", "pair")),
        P(("head", "pair"), None),
        P(),
        P(SEQ_HEAD, None),
        P(SEQ_HEAD, None),
        P(SEQ, None, "pair"),
        P(SEQ, None, "pair"),
        P(SEQ, "pair", None),
    )
    return jax.shard_map(
        body, mesh=split, in_specs=placed, out_specs=P(SEQ_HEAD_PAIR, None), check_vma=False
    )
```

```python
import functools

import jax
import jax.numpy as jnp
from jax import lax
from jax.experimental import pallas as pl
from jax.experimental.pallas import tpu as pltpu
from jax.sharding import Mesh
from jax.sharding import PartitionSpec as P


LANES = 128
CAP = 2
Z = ("zh", "zl")
NEAR = ("zl", "x", "pair")
SEQ = ("zh", "zl", "x")
SEQ_HEAD_PAIR = ("zh", "zl", "x", "head", "pair")
SEQ_HEAD = ("zh", "zl", "x", "head")
SWAP = ((0, 1), (1, 0))
EPSILON = 1e-06


def rms_scale(values, gain_vec):
    mean_sq = jnp.mean(values * values, axis=-1, keepdims=True)
    return values * lax.rsqrt(mean_sq + EPSILON) * gain_vec


def copied(shard, axis):
    return jnp.broadcast_to(shard[None], (lax.axis_size(axis), *shard.shape))


def entering_state(local_state):
    rows, width = local_state.shape
    across = lax.axis_size("x")
    along = lax.axis_size(Z)
    parts = local_state.astype(jnp.bfloat16).reshape(across, rows // across, width)
    parts = lax.all_to_all(parts, "x", 0, 0, tiled=True)
    parts = parts.astype(jnp.float32)
    copies = copied(jnp.sum(parts, axis=0).astype(jnp.bfloat16), Z)
    totals = lax.all_to_all(copies, Z, 0, 0, tiled=True).astype(jnp.float32)
    passed = (jnp.arange(along) < lax.axis_index(Z))[:, None, None]
    running = jnp.sum(jnp.where(passed, totals, 0.0), axis=0)
    entering = []
    for place in range(across):
        entering.append(running.astype(jnp.bfloat16))
        running = running + parts[place]
    back = lax.all_to_all(jnp.stack(entering), "x", 0, 0, tiled=True)
    return back.reshape(rows, width)


def two_terms(values):
    high = lax.reduce_precision(values, exponent_bits=8, mantissa_bits=7)
    return high.astype(jnp.bfloat16), (values - high).astype(jnp.bfloat16)


def with_routing(rows, expert_ids, weights):
    count, top = expert_ids.shape
    high, low = two_terms(weights)
    tail = jnp.concatenate(
        [
            expert_ids.astype(jnp.bfloat16),
            high,
            low,
            jnp.zeros((count, LANES - 3 * top), jnp.bfloat16),
        ],
        axis=1,
    )
    return jnp.concatenate([rows, tail], axis=1)


def slot_kernel(first, packed, slots, high, low, *, block_rows, top):
    count, width = packed.shape[0], slots.shape[1]
    blocks = count // block_rows
    shape = (count, slots.shape[0])
    routing = packed[:, width:].astype(jnp.float32)
    slot = lax.broadcasted_iota(jnp.int32, shape, 1)
    row = lax.broadcasted_iota(jnp.int32, shape, 0)
    wanted = (first[0] + slot // (blocks * CAP)).astype(jnp.float32)
    chosen = jnp.zeros(shape, jnp.float32)
    weight = jnp.zeros(shape, jnp.float32)
    for k in range(top):
        named = routing[:, k : k + 1] == wanted
        value = routing[:, top + k : top + k + 1] + routing[:, 2 * top + k : 2 * top + k + 1]
        chosen = jnp.where(named, 1.0, chosen)
        weight = jnp.where(named, value, weight)
    to_row = lax.broadcasted_iota(jnp.int32, (count, count), 0)
    from_row = lax.broadcasted_iota(jnp.int32, (count, count), 1)
    ahead = (to_row // block_rows == from_row // block_rows) & (from_row < to_row)
    rank = jnp.dot(
        jnp.where(ahead, 1.0, 0.0).astype(jnp.bfloat16),
        chosen.astype(jnp.bfloat16),
        preferred_element_type=jnp.float32,
    )
    fills = (
        (chosen > 0.0)
        & (rank == (slot % CAP).astype(jnp.float32))
        & (slot // CAP % blocks == row // block_rows)
    )
    picks = jnp.where(fills, 1.0, 0.0).astype(jnp.bfloat16)
    slots[...] = lax.dot_general(
        picks, packed[:, :width], (((0,), (0,)), ((), ())), preferred_element_type=jnp.float32
    ).astype(slots.dtype)
    added = jnp.where(fills, weight, 0.0)
    rounded = added.astype(jnp.bfloat16)
    high[...] = rounded
    low[...] = (added - rounded.astype(jnp.float32)).astype(jnp.bfloat16)


def sorted_into_slots(packed, first, experts, block_rows, top):
    count = packed.shape[0]
    slots = experts * (count // block_rows) * CAP
    width = packed.shape[1] - LANES
    on_chip = pl.BlockSpec(memory_space=pltpu.VMEM)
    return pl.pallas_call(
        functools.partial(slot_kernel, block_rows=block_rows, top=top),
        out_shape=(
            jax.ShapeDtypeStruct((slots, width), jnp.bfloat16),
            jax.ShapeDtypeStruct((count, slots), jnp.bfloat16),
            jax.ShapeDtypeStruct((count, slots), jnp.bfloat16),
        ),
        in_specs=[pl.BlockSpec(memory_space=pltpu.SMEM), on_chip],
        out_specs=(on_chip, on_chip, on_chip),
        compiler_params=pltpu.CompilerParams(vmem_limit_bytes=12 * 1024 * 1024),
        name="slots",
    )(first.reshape(1).astype(jnp.int32), packed)


def expert_kernel(core, rows, g0, u0, d0, g1, u1, d1, out, gate_all, up_all, down_all, sems):
    mine = core[0]
    half = g0.shape[2]
    copies = []
    for place, (parts, whole) in enumerate(
        (((g0, g1), gate_all), ((u0, u1), up_all), ((d0, d1), down_all))
    ):
        for index, part in enumerate(parts):
            span = pl.ds(index * half, half)
            view = whole.at[span, :] if whole is down_all else whole.at[:, span]
            copies.append(pltpu.make_async_copy(part.at[mine], view, sems.at[place, index]))
    for copy in copies:
        copy.start()
    values = rows[...]
    copies[0].wait()
    copies[1].wait()
    gate_part = jnp.dot(values, gate_all[...], preferred_element_type=jnp.float32)
    copies[2].wait()
    copies[3].wait()
    up_part = jnp.dot(values, up_all[...], preferred_element_type=jnp.float32)
    hidden = (gate_part / (1.0 + jnp.exp(-gate_part)) * up_part).astype(jnp.bfloat16)
    copies[4].wait()
    copies[5].wait()
    result = jnp.dot(hidden, down_all[...], preferred_element_type=jnp.float32)
    out[...] = result.astype(out.dtype)


def expert(core, rows, own_parts, other_parts):
    _, width, half = own_parts[0].shape
    parts = [
        pltpu.with_memory_space_constraint(part, pltpu.HBM) for part in (*own_parts, *other_parts)
    ]
    in_place = [pl.BlockSpec(memory_space=pl.ANY)] * 6
    return pl.pallas_call(
        expert_kernel,
        out_shape=jax.ShapeDtypeStruct(rows.shape, jnp.bfloat16),
        in_specs=[
            pl.BlockSpec(memory_space=pltpu.SMEM),
            pl.BlockSpec(memory_space=pltpu.VMEM),
            *in_place,
        ],
        out_specs=pl.BlockSpec(memory_space=pltpu.VMEM),
        scratch_shapes=[
            pltpu.VMEM((width, 2 * half), jnp.bfloat16),
            pltpu.VMEM((width, 2 * half), jnp.bfloat16),
            pltpu.VMEM((2 * half, width), jnp.bfloat16),
            pltpu.SemaphoreType.DMA((3, 2)),
        ],
        compiler_params=pltpu.CompilerParams(vmem_limit_bytes=24 * 1024 * 1024),
        name="expert",
    )(core.reshape(1).astype(jnp.int32), rows, *parts)


def layer(
    query_rows,
    all_head_keys,
    value_rows,
    stream,
    attn_gain,
    out_weight,
    moe_gain,
    routes,
    gate_weights,
    w_gate,
    w_up,
    w_down,
):
    length, head_width = query_rows.shape
    block_rows, model_width = stream.shape
    heads = lax.axis_size("head")
    core = lax.axis_index("pair")
    other_weight = lax.ppermute(out_weight, "pair", SWAP)
    local_state = jnp.einsum(
        "tz,td->zd", all_head_keys, value_rows, preferred_element_type=jnp.float32
    )
    other_gate = lax.ppermute(w_gate, "pair", SWAP)
    previous, other_gate = lax.optimization_barrier((entering_state(local_state), other_gate))
    causal = jnp.arange(length)[:, None] >= jnp.arange(length)[None, :]
    scores = jnp.where(
        causal,
        jnp.einsum("tk,sk->ts", query_rows, all_head_keys, preferred_element_type=jnp.float32),
        0.0,
    )
    mixed = jnp.dot(scores, value_rows.astype(jnp.float32))
    mixed = mixed + jnp.dot(query_rows, previous, preferred_element_type=jnp.float32)
    attn_normed = rms_scale(mixed, attn_gain[None, :]).astype(jnp.bfloat16)

    by_core = attn_normed.reshape(heads, 2, block_rows, head_width)
    kept = jnp.where(core == 0, by_core[:, 0], by_core[:, 1]).reshape(-1, head_width)
    given = jnp.where(core == 0, by_core[:, 1], by_core[:, 0]).reshape(-1, head_width)
    taken = lax.ppermute(given, "pair", SWAP)
    partial_rows = jnp.dot(kept, out_weight, preferred_element_type=jnp.float32) + jnp.dot(
        taken, other_weight, preferred_element_type=jnp.float32
    )
    partial_rows = partial_rows.astype(jnp.bfloat16).reshape(heads, block_rows, model_width)
    other_up = lax.ppermute(w_up, "pair", SWAP)
    other_down = lax.ppermute(w_down, "pair", SWAP)
    partial_rows = lax.all_to_all(partial_rows, "head", 0, 0, tiled=True)
    projected = jnp.sum(partial_rows.astype(jnp.float32), axis=0)
    residual = stream.astype(jnp.float32) + projected
    moe_input = rms_scale(residual, moe_gain).astype(jnp.bfloat16)

    my_routes = lax.dynamic_slice_in_dim(routes, core * block_rows, block_rows, 0)
    my_weights = lax.dynamic_slice_in_dim(gate_weights, core * block_rows, block_rows, 0)
    packed = copied(with_routing(moe_input, my_routes, my_weights), "zh")
    packed = lax.all_to_all(packed, "zh", 0, 0, tiled=True)
    blocks = packed.shape[0]
    packed = packed.reshape(blocks * block_rows, -1)
    near = lax.axis_size(NEAR)
    slots, high, low = sorted_into_slots(
        packed, lax.axis_index("zh") * near, near, block_rows, routes.shape[1]
    )
    slots = slots.reshape(near, -1, model_width)
    slots, other_up, other_down = lax.optimization_barrier((slots, other_up, other_down))
    rows = lax.all_to_all(slots, NEAR, 0, 0, tiled=True).reshape(-1, model_width)

    expert_out = expert(
        core, rows, (w_gate, w_up, w_down), (other_gate, other_up, other_down)
    ).reshape(slots.shape)
    returned = lax.all_to_all(expert_out, NEAR, 0, 0, tiled=True)
    returned = returned.reshape(-1, model_width)

    sums = jnp.dot(high, returned, preferred_element_type=jnp.float32)
    sums = sums + jnp.dot(low, returned, preferred_element_type=jnp.float32)
    sums = sums.astype(jnp.bfloat16).reshape(blocks, block_rows, model_width)
    sums = lax.all_to_all(sums, "zh", 0, 0, tiled=True)
    combined = jnp.sum(sums.astype(jnp.float32), axis=0)
    return (residual + combined).astype(jnp.bfloat16)


def solution(mesh):
    split = Mesh(
        mesh.devices.reshape(8, 2, 4, mesh.shape["head"], mesh.shape["pair"]),
        SEQ_HEAD_PAIR,
    )
    placed = (
        P(SEQ, ("head", "pair")),
        P(SEQ, ("head", "pair")),
        P(SEQ, ("head", "pair")),
        P(SEQ_HEAD_PAIR, None),
        P(("head", "pair")),
        P(("head", "pair"), None),
        P(),
        P(SEQ_HEAD, None),
        P(SEQ_HEAD, None),
        P(SEQ, None, "pair"),
        P(SEQ, None, "pair"),
        P(SEQ, "pair", None),
    )
    return jax.shard_map(
        layer, mesh=split, in_specs=placed, out_specs=P(SEQ_HEAD_PAIR, None), check_vma=False
    )
```

```python
import functools

import jax
import jax.numpy as jnp
from jax import lax
from jax.experimental import pallas as pl
from jax.experimental.pallas import tpu as pltpu
from jax.sharding import Mesh
from jax.sharding import PartitionSpec as P


LANES = 128
CAP = 2
Z = ("zh", "zl")
NEAR = ("zl", "x", "pair")
SEQ = ("zh", "zl", "x")
SEQ_HEAD_PAIR = ("zh", "zl", "x", "head", "pair")
SEQ_HEAD = ("zh", "zl", "x", "head")
SWAP = ((0, 1), (1, 0))
EPSILON = 1e-06


def rms_scale(values, gain_vec):
    mean_sq = jnp.mean(values * values, axis=-1, keepdims=True)
    return values * lax.rsqrt(mean_sq + EPSILON) * gain_vec


def copied(shard, axis):
    return jnp.broadcast_to(shard[None], (lax.axis_size(axis), *shard.shape))


def entering_state(local_state):
    rows, width = local_state.shape
    across = lax.axis_size("x")
    along = lax.axis_size(Z)
    parts = local_state.astype(jnp.bfloat16).reshape(across, rows // across, width)
    parts = lax.all_to_all(parts, "x", 0, 0, tiled=True)
    parts = parts.astype(jnp.float32)
    copies = copied(jnp.sum(parts, axis=0).astype(jnp.bfloat16), Z)
    totals = lax.all_to_all(copies, Z, 0, 0, tiled=True).astype(jnp.float32)
    passed = (jnp.arange(along) < lax.axis_index(Z))[:, None, None]
    running = jnp.sum(jnp.where(passed, totals, 0.0), axis=0)
    entering = []
    for place in range(across):
        entering.append(running.astype(jnp.bfloat16))
        running = running + parts[place]
    entering = jnp.repeat(jnp.stack(entering), lax.axis_size("pair"), axis=0)
    back = lax.all_to_all(entering, ("x", "pair"), 0, 0, tiled=True)
    back = back.reshape(across, lax.axis_size("pair"), rows // across, width)
    return jnp.moveaxis(back, 1, 0).reshape(-1, rows, width)


def two_terms(values):
    high = lax.reduce_precision(values, exponent_bits=8, mantissa_bits=7)
    return high.astype(jnp.bfloat16), (values - high).astype(jnp.bfloat16)


def routing_tail(expert_ids, weights):
    count, top = expert_ids.shape
    high, low = two_terms(weights)
    unused = jnp.zeros((count, LANES - 3 * top), jnp.bfloat16)
    return jnp.concatenate([expert_ids.astype(jnp.bfloat16), high, low, unused], axis=1)


def attend_kernel(
    core, q0, q1, parts0, parts1, gain1, w1, entering, gain_in, w_in, out, gain0, w0, sems, *, block_rows
):
    copies = [
        pltpu.make_async_copy(gain_in, gain0, sems.at[0]),
        pltpu.make_async_copy(w_in, w0, sems.at[1]),
    ]
    for copy in copies:
        copy.start()
    mine = core[0]
    count, length = q0.shape[0], parts0.shape[1]
    place = lax.broadcasted_iota(jnp.int32, (count, length), 0)
    row = place // block_rows * 2 * block_rows + mine * block_rows + place % block_rows
    causal = lax.broadcasted_iota(jnp.int32, (count, length), 1) <= row

    def scaled(q, parts, state):
        scores = lax.dot_general(
            q[...], parts[1], (((1,), (1,)), ((), ())), preferred_element_type=jnp.float32
        )
        scores = jnp.where(causal, scores, 0.0)
        high = scores.astype(jnp.bfloat16)
        low = (scores - high.astype(jnp.float32)).astype(jnp.bfloat16)
        mixed = jnp.dot(high, parts[2], preferred_element_type=jnp.float32)
        mixed = mixed + jnp.dot(low, parts[2], preferred_element_type=jnp.float32)
        mixed = mixed + jnp.dot(q[...], state, preferred_element_type=jnp.float32)
        return rms_scale(mixed, jnp.ones_like(gain1[...]))

    rows1 = (scaled(q1, parts1, entering[1 - mine]) * gain1[...]).astype(jnp.bfloat16)
    rows0 = scaled(q0, parts0, entering[mine])
    for copy in copies:
        copy.wait()
    rows0 = (rows0 * gain0[...]).astype(jnp.bfloat16)
    total = jnp.dot(rows1, w1[...], preferred_element_type=jnp.float32)
    total = total + jnp.dot(rows0, w0[...], preferred_element_type=jnp.float32)
    out[...] = total.astype(out.dtype)


def attended(core, own, other, entering, block_rows):
    def kept(parts):
        by_core = parts[0].reshape(-1, 2, block_rows, parts.shape[2])
        return jnp.where(core == 0, by_core[:, 0], by_core[:, 1]).reshape(-1, parts.shape[2])

    own_parts, own_gain, own_weight = own
    other_parts, other_gain, other_weight = other
    query = kept(own_parts)
    far = [pltpu.with_memory_space_constraint(array, pltpu.HBM) for array in (own_gain, own_weight)]
    on_chip = pl.BlockSpec(memory_space=pltpu.VMEM)
    in_place = pl.BlockSpec(memory_space=pl.ANY)
    return pl.pallas_call(
        functools.partial(attend_kernel, block_rows=block_rows),
        out_shape=jax.ShapeDtypeStruct((query.shape[0], own_weight.shape[1]), jnp.bfloat16),
        in_specs=[pl.BlockSpec(memory_space=pltpu.SMEM)] + [on_chip] * 7 + [in_place] * 2,
        out_specs=on_chip,
        scratch_shapes=[
            pltpu.VMEM(own_gain.shape, jnp.float32),
            pltpu.VMEM(own_weight.shape, jnp.bfloat16),
            pltpu.SemaphoreType.DMA((2,)),
        ],
        compiler_params=pltpu.CompilerParams(vmem_limit_bytes=12 * 1024 * 1024),
        name="attend",
    )(
        core.reshape(1).astype(jnp.int32),
        query,
        kept(other_parts),
        own_parts,
        other_parts,
        other_gain,
        other_weight,
        entering,
        *far,
    )


def norm_kernel(parts, stream, gain, tail, residual, packed):
    width = stream.shape[1]
    total = stream[...].astype(jnp.float32) + jnp.sum(parts[...].astype(jnp.float32), axis=0)
    residual[...] = total
    rows = rms_scale(total, gain[...]).astype(packed.dtype)
    for copy in range(packed.shape[0]):
        packed[copy, :, :width] = rows
        packed[copy, :, width:] = tail[...]


def normed_copies(parts, stream, gain, tail, copies):
    rows, width = stream.shape
    on_chip = pl.BlockSpec(memory_space=pltpu.VMEM)
    return pl.pallas_call(
        norm_kernel,
        out_shape=(
            jax.ShapeDtypeStruct((rows, width), jnp.float32),
            jax.ShapeDtypeStruct((copies, rows, width + tail.shape[1]), jnp.bfloat16),
        ),
        in_specs=[on_chip] * 4,
        out_specs=(on_chip, on_chip),
        compiler_params=pltpu.CompilerParams(vmem_limit_bytes=8 * 1024 * 1024),
        name="norm",
    )(parts, stream, gain.reshape(1, -1), tail)


def slot_kernel(first, packed, slots, high, low, *, block_rows, top):
    count, width = packed.shape[0], slots.shape[1]
    blocks = count // block_rows
    shape = (count, slots.shape[0])
    routing = packed[:, width:].astype(jnp.float32)
    slot = lax.broadcasted_iota(jnp.int32, shape, 1)
    row = lax.broadcasted_iota(jnp.int32, shape, 0)
    wanted = (first[0] + slot // (blocks * CAP)).astype(jnp.float32)
    chosen = jnp.zeros(shape, jnp.float32)
    weight = jnp.zeros(shape, jnp.float32)
    for k in range(top):
        named = routing[:, k : k + 1] == wanted
        value = routing[:, top + k : top + k + 1] + routing[:, 2 * top + k : 2 * top + k + 1]
        chosen = jnp.where(named, 1.0, chosen)
        weight = jnp.where(named, value, weight)
    to_row = lax.broadcasted_iota(jnp.int32, (count, count), 0)
    from_row = lax.broadcasted_iota(jnp.int32, (count, count), 1)
    ahead = (to_row // block_rows == from_row // block_rows) & (from_row < to_row)
    rank = jnp.dot(
        jnp.where(ahead, 1.0, 0.0).astype(jnp.bfloat16),
        chosen.astype(jnp.bfloat16),
        preferred_element_type=jnp.float32,
    )
    fills = (
        (chosen > 0.0)
        & (rank == (slot % CAP).astype(jnp.float32))
        & (slot // CAP % blocks == row // block_rows)
    )
    picks = jnp.where(fills, 1.0, 0.0).astype(jnp.bfloat16)
    slots[...] = lax.dot_general(
        picks, packed[:, :width], (((0,), (0,)), ((), ())), preferred_element_type=jnp.float32
    ).astype(slots.dtype)
    added = jnp.where(fills, weight, 0.0)
    rounded = added.astype(jnp.bfloat16)
    high[...] = rounded
    low[...] = (added - rounded.astype(jnp.float32)).astype(jnp.bfloat16)


def sorted_into_slots(packed, first, experts, block_rows, top):
    count = packed.shape[0]
    slots = experts * (count // block_rows) * CAP
    width = packed.shape[1] - LANES
    on_chip = pl.BlockSpec(memory_space=pltpu.VMEM)
    return pl.pallas_call(
        functools.partial(slot_kernel, block_rows=block_rows, top=top),
        out_shape=(
            jax.ShapeDtypeStruct((slots, width), jnp.bfloat16),
            jax.ShapeDtypeStruct((count, slots), jnp.bfloat16),
            jax.ShapeDtypeStruct((count, slots), jnp.bfloat16),
        ),
        in_specs=[pl.BlockSpec(memory_space=pltpu.SMEM), on_chip],
        out_specs=(on_chip, on_chip, on_chip),
        compiler_params=pltpu.CompilerParams(vmem_limit_bytes=12 * 1024 * 1024),
        name="slots",
    )(first.reshape(1).astype(jnp.int32), packed)


def expert_kernel(core, rows, g0, u0, d0, g1, u1, d1, out, gate_all, up_all, down_all, sems):
    mine = core[0]
    half = g0.shape[2]
    copies = []
    for place, (parts, whole) in enumerate(
        (((g0, g1), gate_all), ((u0, u1), up_all), ((d0, d1), down_all))
    ):
        for index, part in enumerate(parts):
            span = pl.ds(index * half, half)
            view = whole.at[span, :] if whole is down_all else whole.at[:, span]
            copies.append(pltpu.make_async_copy(part.at[mine], view, sems.at[place, index]))
    for copy in copies:
        copy.start()
    values = rows[...]
    copies[0].wait()
    copies[1].wait()
    gate_part = jnp.dot(values, gate_all[...], preferred_element_type=jnp.float32)
    copies[2].wait()
    copies[3].wait()
    up_part = jnp.dot(values, up_all[...], preferred_element_type=jnp.float32)
    hidden = (gate_part / (1.0 + jnp.exp(-gate_part)) * up_part).astype(jnp.bfloat16)
    copies[4].wait()
    copies[5].wait()
    result = jnp.dot(hidden, down_all[...], preferred_element_type=jnp.float32)
    out[...] = result.astype(out.dtype)


def expert(core, rows, own_parts, other_parts):
    _, width, half = own_parts[0].shape
    parts = [
        pltpu.with_memory_space_constraint(part, pltpu.HBM) for part in (*own_parts, *other_parts)
    ]
    in_place = [pl.BlockSpec(memory_space=pl.ANY)] * 6
    return pl.pallas_call(
        expert_kernel,
        out_shape=jax.ShapeDtypeStruct(rows.shape, jnp.bfloat16),
        in_specs=[
            pl.BlockSpec(memory_space=pltpu.SMEM),
            pl.BlockSpec(memory_space=pltpu.VMEM),
            *in_place,
        ],
        out_specs=pl.BlockSpec(memory_space=pltpu.VMEM),
        scratch_shapes=[
            pltpu.VMEM((width, 2 * half), jnp.bfloat16),
            pltpu.VMEM((width, 2 * half), jnp.bfloat16),
            pltpu.VMEM((2 * half, width), jnp.bfloat16),
            pltpu.SemaphoreType.DMA((3, 2)),
        ],
        compiler_params=pltpu.CompilerParams(vmem_limit_bytes=24 * 1024 * 1024),
        name="expert",
    )(core.reshape(1).astype(jnp.int32), rows, *parts)


def layer(
    query_rows,
    all_head_keys,
    value_rows,
    stream,
    attn_gain,
    out_weight,
    moe_gain,
    routes,
    gate_weights,
    w_gate,
    w_up,
    w_down,
):
    block_rows, model_width = stream.shape
    heads = lax.axis_size("head")
    core = lax.axis_index("pair")
    other_weight = lax.ppermute(out_weight, "pair", SWAP)
    local_state = jnp.einsum(
        "tz,td->zd", all_head_keys, value_rows, preferred_element_type=jnp.float32
    )
    other_gate = lax.ppermute(w_gate, "pair", SWAP)
    own_parts = jnp.stack([query_rows, all_head_keys, value_rows])
    other_parts = lax.ppermute(own_parts, "pair", SWAP)
    other_gain = lax.ppermute(attn_gain.reshape(1, -1), "pair", SWAP)
    previous = entering_state(local_state)
    partial_rows = attended(
        core,
        (own_parts, attn_gain.reshape(1, -1), out_weight),
        (other_parts, other_gain, other_weight),
        previous,
        block_rows,
    ).reshape(heads, block_rows, model_width)
    other_up = lax.ppermute(w_up, "pair", SWAP)
    other_down = lax.ppermute(w_down, "pair", SWAP)
    partial_rows = lax.all_to_all(partial_rows, "head", 0, 0, tiled=True)
    my_routes = lax.dynamic_slice_in_dim(routes, core * block_rows, block_rows, 0)
    my_weights = lax.dynamic_slice_in_dim(gate_weights, core * block_rows, block_rows, 0)
    residual, packed = normed_copies(
        partial_rows, stream, moe_gain, routing_tail(my_routes, my_weights), lax.axis_size("zh")
    )
    packed = lax.all_to_all(packed, "zh", 0, 0, tiled=True)
    blocks = packed.shape[0]
    packed = packed.reshape(blocks * block_rows, -1)
    near = lax.axis_size(NEAR)
    slots, high, low = sorted_into_slots(
        packed, lax.axis_index("zh") * near, near, block_rows, routes.shape[1]
    )
    slots = slots.reshape(near, -1, model_width)
    slots, other_gate, other_up, other_down = lax.optimization_barrier(
        (slots, other_gate, other_up, other_down)
    )
    rows = lax.all_to_all(slots, NEAR, 0, 0, tiled=True).reshape(-1, model_width)

    expert_out = expert(
        core, rows, (w_gate, w_up, w_down), (other_gate, other_up, other_down)
    ).reshape(slots.shape)
    returned = lax.all_to_all(expert_out, NEAR, 0, 0, tiled=True)
    returned = returned.reshape(-1, model_width)

    sums = jnp.dot(high, returned, preferred_element_type=jnp.float32)
    sums = sums + jnp.dot(low, returned, preferred_element_type=jnp.float32)
    sums = sums.astype(jnp.bfloat16).reshape(blocks, block_rows, model_width)
    sums = lax.all_to_all(sums, "zh", 0, 0, tiled=True)
    combined = jnp.sum(sums.astype(jnp.float32), axis=0)
    return (residual + combined).astype(jnp.bfloat16)


def solution(mesh):
    split = Mesh(
        mesh.devices.reshape(8, 2, 4, mesh.shape["head"], mesh.shape["pair"]),
        SEQ_HEAD_PAIR,
    )
    placed = (
        P(SEQ, ("head", "pair")),
        P(SEQ, ("head", "pair")),
        P(SEQ, ("head", "pair")),
        P(SEQ_HEAD_PAIR, None),
        P(("head", "pair")),
        P(("head", "pair"), None),
        P(),
        P(SEQ_HEAD, None),
        P(SEQ_HEAD, None),
        P(SEQ, None, "pair"),
        P(SEQ, None, "pair"),
        P(SEQ, "pair", None),
    )
    return jax.shard_map(
        layer, mesh=split, in_specs=placed, out_specs=P(SEQ_HEAD_PAIR, None), check_vma=False
    )
```

```python
import functools

import jax
import jax.numpy as jnp
from jax import lax
from jax.experimental import pallas as pl
from jax.experimental.pallas import tpu as pltpu
from jax.sharding import Mesh
from jax.sharding import PartitionSpec as P


LANES = 128
CAP = 2
Z = ("zh", "zl")
NEAR = ("zl", "x", "pair")
SEQ = ("zh", "zl", "x")
SEQ_HEAD_PAIR = ("zh", "zl", "x", "head", "pair")
SEQ_HEAD = ("zh", "zl", "x", "head")
SWAP = ((0, 1), (1, 0))
EPSILON = 1e-06


def rms_scale(values, gain_vec):
    mean_sq = jnp.mean(values * values, axis=-1, keepdims=True)
    return values * lax.rsqrt(mean_sq + EPSILON) * gain_vec


def copied(shard, axis):
    return jnp.broadcast_to(shard[None], (lax.axis_size(axis), *shard.shape))


def entering_state(local_state):
    rows, width = local_state.shape
    across = lax.axis_size("x")
    along = lax.axis_size(Z)
    parts = local_state.astype(jnp.bfloat16).reshape(across, rows // across, width)
    parts = lax.all_to_all(parts, "x", 0, 0, tiled=True)
    parts = parts.astype(jnp.float32)
    copies = copied(jnp.sum(parts, axis=0).astype(jnp.bfloat16), Z)
    totals = lax.all_to_all(copies, Z, 0, 0, tiled=True).astype(jnp.float32)
    passed = (jnp.arange(along) < lax.axis_index(Z))[:, None, None]
    running = jnp.sum(jnp.where(passed, totals, 0.0), axis=0)
    entering = []
    for place in range(across):
        entering.append(running.astype(jnp.bfloat16))
        running = running + parts[place]
    entering = jnp.repeat(jnp.stack(entering), lax.axis_size("pair"), axis=0)
    back = lax.all_to_all(entering, ("x", "pair"), 0, 0, tiled=True)
    back = back.reshape(across, lax.axis_size("pair"), rows // across, width)
    return jnp.moveaxis(back, 1, 0).reshape(-1, rows, width)


def two_terms(values):
    high = lax.reduce_precision(values, exponent_bits=8, mantissa_bits=7)
    return high.astype(jnp.bfloat16), (values - high).astype(jnp.bfloat16)


def routing_tail(expert_ids, weights):
    count, top = expert_ids.shape
    high, low = two_terms(weights)
    unused = jnp.zeros((count, LANES - 3 * top), jnp.bfloat16)
    return jnp.concatenate([expert_ids.astype(jnp.bfloat16), high, low, unused], axis=1)


def in_block_kernel(core, q0, q1, parts0, parts1, mixed, *, block_rows):
    count, length = q0.shape[0], parts0.shape[1]
    place = lax.broadcasted_iota(jnp.int32, (count, length), 0)
    row = place // block_rows * 2 * block_rows + core[0] * block_rows + place % block_rows
    causal = lax.broadcasted_iota(jnp.int32, (count, length), 1) <= row
    for index, (q, parts) in enumerate(((q0, parts0), (q1, parts1))):
        scores = lax.dot_general(
            q[...], parts[1], (((1,), (1,)), ((), ())), preferred_element_type=jnp.float32
        )
        scores = jnp.where(causal, scores, 0.0)
        high = scores.astype(jnp.bfloat16)
        low = (scores - high.astype(jnp.float32)).astype(jnp.bfloat16)
        total = jnp.dot(high, parts[2], preferred_element_type=jnp.float32)
        mixed[index] = total + jnp.dot(low, parts[2], preferred_element_type=jnp.float32)


def attend_kernel(
    core, q0, q1, mixed, gain1, w1, entering, gain_in, w_in, out, gain0, w0, sems
):
    copies = [
        pltpu.make_async_copy(gain_in, gain0, sems.at[0]),
        pltpu.make_async_copy(w_in, w0, sems.at[1]),
    ]
    for copy in copies:
        copy.start()
    mine = core[0]

    def scaled(q, index, state):
        total = mixed[index] + jnp.dot(q[...], state, preferred_element_type=jnp.float32)
        return rms_scale(total, jnp.ones_like(gain1[...]))

    rows1 = (scaled(q1, 1, entering[1 - mine]) * gain1[...]).astype(jnp.bfloat16)
    rows0 = scaled(q0, 0, entering[mine])
    for copy in copies:
        copy.wait()
    rows0 = (rows0 * gain0[...]).astype(jnp.bfloat16)
    total = jnp.dot(rows1, w1[...], preferred_element_type=jnp.float32)
    total = total + jnp.dot(rows0, w0[...], preferred_element_type=jnp.float32)
    out[...] = total.astype(out.dtype)


def in_block(core, own_parts, other_parts, block_rows):
    def kept(parts):
        by_core = parts[0].reshape(-1, 2, block_rows, parts.shape[2])
        return jnp.where(core == 0, by_core[:, 0], by_core[:, 1]).reshape(-1, parts.shape[2])

    queries = (kept(own_parts), kept(other_parts))
    on_chip = pl.BlockSpec(memory_space=pltpu.VMEM)
    mixed = pl.pallas_call(
        functools.partial(in_block_kernel, block_rows=block_rows),
        out_shape=jax.ShapeDtypeStruct((2, *queries[0].shape), jnp.float32),
        in_specs=[pl.BlockSpec(memory_space=pltpu.SMEM)] + [on_chip] * 4,
        out_specs=on_chip,
        compiler_params=pltpu.CompilerParams(vmem_limit_bytes=8 * 1024 * 1024),
        name="in_block",
    )(core.reshape(1).astype(jnp.int32), *queries, own_parts, other_parts)
    return queries, mixed


def attended(core, queries, mixed, own, other, entering):
    own_gain, own_weight = own
    far = [pltpu.with_memory_space_constraint(array, pltpu.HBM) for array in own]
    on_chip = pl.BlockSpec(memory_space=pltpu.VMEM)
    in_place = pl.BlockSpec(memory_space=pl.ANY)
    return pl.pallas_call(
        attend_kernel,
        out_shape=jax.ShapeDtypeStruct((mixed.shape[1], own_weight.shape[1]), jnp.bfloat16),
        in_specs=[pl.BlockSpec(memory_space=pltpu.SMEM)] + [on_chip] * 6 + [in_place] * 2,
        out_specs=on_chip,
        scratch_shapes=[
            pltpu.VMEM(own_gain.shape, jnp.float32),
            pltpu.VMEM(own_weight.shape, jnp.bfloat16),
            pltpu.SemaphoreType.DMA((2,)),
        ],
        compiler_params=pltpu.CompilerParams(vmem_limit_bytes=12 * 1024 * 1024),
        name="attend",
    )(core.reshape(1).astype(jnp.int32), *queries, mixed, *other, entering, *far)


def norm_kernel(parts, stream, gain, tail, residual, packed):
    width = stream.shape[1]
    total = stream[...].astype(jnp.float32) + jnp.sum(parts[...].astype(jnp.float32), axis=0)
    residual[...] = total
    rows = rms_scale(total, gain[...]).astype(packed.dtype)
    for copy in range(packed.shape[0]):
        packed[copy, :, :width] = rows
        packed[copy, :, width:] = tail[...]


def normed_copies(parts, stream, gain, tail, copies):
    rows, width = stream.shape
    on_chip = pl.BlockSpec(memory_space=pltpu.VMEM)
    return pl.pallas_call(
        norm_kernel,
        out_shape=(
            jax.ShapeDtypeStruct((rows, width), jnp.float32),
            jax.ShapeDtypeStruct((copies, rows, width + tail.shape[1]), jnp.bfloat16),
        ),
        in_specs=[on_chip] * 4,
        out_specs=(on_chip, on_chip),
        compiler_params=pltpu.CompilerParams(vmem_limit_bytes=8 * 1024 * 1024),
        name="norm",
    )(parts, stream, gain.reshape(1, -1), tail)


def slot_kernel(first, packed, slots, high, low, *, block_rows, top):
    count, width = packed.shape[0], slots.shape[1]
    blocks = count // block_rows
    shape = (count, slots.shape[0])
    routing = packed[:, width:].astype(jnp.float32)
    slot = lax.broadcasted_iota(jnp.int32, shape, 1)
    row = lax.broadcasted_iota(jnp.int32, shape, 0)
    wanted = (first[0] + slot // (blocks * CAP)).astype(jnp.float32)
    chosen = jnp.zeros(shape, jnp.float32)
    weight = jnp.zeros(shape, jnp.float32)
    for k in range(top):
        named = routing[:, k : k + 1] == wanted
        value = routing[:, top + k : top + k + 1] + routing[:, 2 * top + k : 2 * top + k + 1]
        chosen = jnp.where(named, 1.0, chosen)
        weight = jnp.where(named, value, weight)
    to_row = lax.broadcasted_iota(jnp.int32, (count, count), 0)
    from_row = lax.broadcasted_iota(jnp.int32, (count, count), 1)
    ahead = (to_row // block_rows == from_row // block_rows) & (from_row < to_row)
    rank = jnp.dot(
        jnp.where(ahead, 1.0, 0.0).astype(jnp.bfloat16),
        chosen.astype(jnp.bfloat16),
        preferred_element_type=jnp.float32,
    )
    fills = (
        (chosen > 0.0)
        & (rank == (slot % CAP).astype(jnp.float32))
        & (slot // CAP % blocks == row // block_rows)
    )
    picks = jnp.where(fills, 1.0, 0.0).astype(jnp.bfloat16)
    slots[...] = lax.dot_general(
        picks, packed[:, :width], (((0,), (0,)), ((), ())), preferred_element_type=jnp.float32
    ).astype(slots.dtype)
    added = jnp.where(fills, weight, 0.0)
    rounded = added.astype(jnp.bfloat16)
    high[...] = rounded
    low[...] = (added - rounded.astype(jnp.float32)).astype(jnp.bfloat16)


def sorted_into_slots(packed, first, experts, block_rows, top):
    count = packed.shape[0]
    slots = experts * (count // block_rows) * CAP
    width = packed.shape[1] - LANES
    on_chip = pl.BlockSpec(memory_space=pltpu.VMEM)
    return pl.pallas_call(
        functools.partial(slot_kernel, block_rows=block_rows, top=top),
        out_shape=(
            jax.ShapeDtypeStruct((slots, width), jnp.bfloat16),
            jax.ShapeDtypeStruct((count, slots), jnp.bfloat16),
            jax.ShapeDtypeStruct((count, slots), jnp.bfloat16),
        ),
        in_specs=[pl.BlockSpec(memory_space=pltpu.SMEM), on_chip],
        out_specs=(on_chip, on_chip, on_chip),
        compiler_params=pltpu.CompilerParams(vmem_limit_bytes=12 * 1024 * 1024),
        name="slots",
    )(first.reshape(1).astype(jnp.int32), packed)


def expert_kernel(core, rows, g0, u0, d0, g1, u1, d1, out, gate_all, up_all, down_all, sems):
    mine = core[0]
    half = g0.shape[2]
    copies = []
    for place, (parts, whole) in enumerate(
        (((g0, g1), gate_all), ((u0, u1), up_all), ((d0, d1), down_all))
    ):
        for index, part in enumerate(parts):
            span = pl.ds(index * half, half)
            view = whole.at[span, :] if whole is down_all else whole.at[:, span]
            copies.append(pltpu.make_async_copy(part.at[mine], view, sems.at[place, index]))
    for copy in copies:
        copy.start()
    values = rows[...]
    copies[0].wait()
    copies[1].wait()
    gate_part = jnp.dot(values, gate_all[...], preferred_element_type=jnp.float32)
    copies[2].wait()
    copies[3].wait()
    up_part = jnp.dot(values, up_all[...], preferred_element_type=jnp.float32)
    hidden = (gate_part / (1.0 + jnp.exp(-gate_part)) * up_part).astype(jnp.bfloat16)
    copies[4].wait()
    copies[5].wait()
    result = jnp.dot(hidden, down_all[...], preferred_element_type=jnp.float32)
    out[...] = result.astype(out.dtype)


def expert(core, rows, own_parts, other_parts):
    _, width, half = own_parts[0].shape
    parts = [
        pltpu.with_memory_space_constraint(part, pltpu.HBM) for part in (*own_parts, *other_parts)
    ]
    in_place = [pl.BlockSpec(memory_space=pl.ANY)] * 6
    return pl.pallas_call(
        expert_kernel,
        out_shape=jax.ShapeDtypeStruct(rows.shape, jnp.bfloat16),
        in_specs=[
            pl.BlockSpec(memory_space=pltpu.SMEM),
            pl.BlockSpec(memory_space=pltpu.VMEM),
            *in_place,
        ],
        out_specs=pl.BlockSpec(memory_space=pltpu.VMEM),
        scratch_shapes=[
            pltpu.VMEM((width, 2 * half), jnp.bfloat16),
            pltpu.VMEM((width, 2 * half), jnp.bfloat16),
            pltpu.VMEM((2 * half, width), jnp.bfloat16),
            pltpu.SemaphoreType.DMA((3, 2)),
        ],
        compiler_params=pltpu.CompilerParams(vmem_limit_bytes=24 * 1024 * 1024),
        name="expert",
    )(core.reshape(1).astype(jnp.int32), rows, *parts)


def layer(
    query_rows,
    all_head_keys,
    value_rows,
    stream,
    attn_gain,
    out_weight,
    moe_gain,
    routes,
    gate_weights,
    w_gate,
    w_up,
    w_down,
):
    block_rows, model_width = stream.shape
    heads = lax.axis_size("head")
    core = lax.axis_index("pair")
    other_weight = lax.ppermute(out_weight, "pair", SWAP)
    local_state = jnp.einsum(
        "tz,td->zd", all_head_keys, value_rows, preferred_element_type=jnp.float32
    )
    other_gate = lax.ppermute(w_gate, "pair", SWAP)
    own_parts = jnp.stack([query_rows, all_head_keys, value_rows])
    other_parts = lax.ppermute(own_parts, "pair", SWAP)
    other_gain = lax.ppermute(attn_gain.reshape(1, -1), "pair", SWAP)
    queries, mixed = in_block(core, own_parts, other_parts, block_rows)
    previous = entering_state(local_state)
    partial_rows = attended(
        core,
        queries,
        mixed,
        (attn_gain.reshape(1, -1), out_weight),
        (other_gain, other_weight),
        previous,
    ).reshape(heads, block_rows, model_width)
    other_up = lax.ppermute(w_up, "pair", SWAP)
    other_down = lax.ppermute(w_down, "pair", SWAP)
    partial_rows = lax.all_to_all(partial_rows, "head", 0, 0, tiled=True)
    my_routes = lax.dynamic_slice_in_dim(routes, core * block_rows, block_rows, 0)
    my_weights = lax.dynamic_slice_in_dim(gate_weights, core * block_rows, block_rows, 0)
    residual, packed = normed_copies(
        partial_rows, stream, moe_gain, routing_tail(my_routes, my_weights), lax.axis_size("zh")
    )
    packed = lax.all_to_all(packed, "zh", 0, 0, tiled=True)
    blocks = packed.shape[0]
    packed = packed.reshape(blocks * block_rows, -1)
    near = lax.axis_size(NEAR)
    slots, high, low = sorted_into_slots(
        packed, lax.axis_index("zh") * near, near, block_rows, routes.shape[1]
    )
    slots = slots.reshape(near, -1, model_width)
    slots, other_gate, other_up, other_down = lax.optimization_barrier(
        (slots, other_gate, other_up, other_down)
    )
    rows = lax.all_to_all(slots, NEAR, 0, 0, tiled=True).reshape(-1, model_width)

    expert_out = expert(
        core, rows, (w_gate, w_up, w_down), (other_gate, other_up, other_down)
    ).reshape(slots.shape)
    returned = lax.all_to_all(expert_out, NEAR, 0, 0, tiled=True)
    returned = returned.reshape(-1, model_width)

    sums = jnp.dot(high, returned, preferred_element_type=jnp.float32)
    sums = sums + jnp.dot(low, returned, preferred_element_type=jnp.float32)
    sums = sums.astype(jnp.bfloat16).reshape(blocks, block_rows, model_width)
    sums = lax.all_to_all(sums, "zh", 0, 0, tiled=True)
    combined = jnp.sum(sums.astype(jnp.float32), axis=0)
    return (residual + combined).astype(jnp.bfloat16)


def solution(mesh):
    split = Mesh(
        mesh.devices.reshape(8, 2, 4, mesh.shape["head"], mesh.shape["pair"]),
        SEQ_HEAD_PAIR,
    )
    placed = (
        P(SEQ, ("head", "pair")),
        P(SEQ, ("head", "pair")),
        P(SEQ, ("head", "pair")),
        P(SEQ_HEAD_PAIR, None),
        P(("head", "pair")),
        P(("head", "pair"), None),
        P(),
        P(SEQ_HEAD, None),
        P(SEQ_HEAD, None),
        P(SEQ, None, "pair"),
        P(SEQ, None, "pair"),
        P(SEQ, "pair", None),
    )
    return jax.shard_map(
        layer, mesh=split, in_specs=placed, out_specs=P(SEQ_HEAD_PAIR, None), check_vma=False
    )
```
